32 devices in a mesh: seq: 8 (over y, x, core), tp: 4 (over z).
Axes of the slice: x: 2, y: 2, z: 4, core: 2. Of those that a mesh axis runs over, the one named last changes fastest.
Arguments:
- hidden: bfloat16 [10240, 8192], P('seq', 'tp'), may hold values from -6 to 6
- queries: bfloat16 [10240, 8192], P('seq', 'tp'), may hold values from -8 to 8
- keys_values: bfloat16 [2, 10240, 1024], P(None, 'seq', 'tp'), may hold values from -8 to 8
- w_router: bfloat16 [8192], P('tp'), may hold values from -0.0625 to 0.0625
- routed: int32 [8, 160], P('seq'), may hold values from 0 to 1279, as said below
- counts: int32 [8], replicated, may hold values from 1 to 160, 800 in all
- grad_out: bfloat16 [1280, 8192], P('seq', 'tp'), may hold values from -6 to 6
Outputs:
- branch_out: bfloat16 [1280, 8192], P('seq', 'tp')
- grad_queries: bfloat16 [1280, 8192], P('seq', 'tp')
- grad_keys_values: bfloat16 [2, 1280, 1024], P(None, 'seq', 'tp')
- grad_router: float32 [8192], P('tp')
The draws below stay inside these ranges and needn't reach their ends.
Inputs may be any that keep to these rules, and one draw needn't show every extreme that they name: Each row lists 160 different positions of one shard's tokens in increasing order; the first counts entries of a row are the shard's routed tokens. `counts`: each shard has at least one live slot and one shard has all 160.
All inputs are finite; a program needn't handle non-finite values.
Results may differ from the reference program's by a relative error of at most 0.03.
Values may be sent and summed in bfloat16 or wider, within the bound.
No kernel may reach another device: no remote copies, remote signals or barrier semaphores. Data moves between devices by JAX's collectives and lax.ppermute only.
A program may use at most 128 MiB of HBM per device.

```python
import math
import jax
import jax.numpy as jnp
import numpy as np
from jax import lax

D = 8192
QUERY_HEADS = 64
HK = 8
HEAD_WIDTH = 128
TOK_DEV = 1280
SLOT_LIMIT = 160
SHARDS = 8
TOKENS = 10240
ROUTED = 1280


def draw_queries(key, part):
    result = jnp.clip(jax.random.normal(jax.random.fold_in(key, 1), (TOKENS, QUERY_HEADS * HEAD_WIDTH), jnp.float32), -6.0, 6.0)
    return result.astype(jnp.bfloat16)


def draw_keys_values(key, part):
    key_part = jnp.clip(jax.random.normal(jax.random.fold_in(key, 2), (TOKENS, HK * HEAD_WIDTH), jnp.float32), -6.0, 6.0)
    value_part = jnp.clip(jax.random.normal(jax.random.fold_in(key, 3), (TOKENS, HK * HEAD_WIDTH), jnp.float32), -6.0, 6.0)
    return jnp.stack([key_part, value_part]).astype(jnp.bfloat16)


def draw_routed(key, part):
    ranking = jax.random.randint(key, (SHARDS, TOK_DEV), 0, 2 ** 18) * TOK_DEV + jnp.arange(TOK_DEV, dtype=jnp.int32)[None, :]
    ranking = ranking.at[0, TOK_DEV - 1].set(2 ** 30)
    ranking = ranking.at[1, 0].set(2 ** 30)
    chosen = jax.lax.top_k(ranking, SLOT_LIMIT)[1]
    return jnp.sort(chosen, axis=1).astype(jnp.int32)


def shard_levels(key, shape, shards, smallest, top_value):
    level = 1.0
    for position, shards_of in shards:
        heights = jax.random.uniform(jax.random.fold_in(jax.random.fold_in(key, 6), position), (shards_of,), jnp.float32, smallest / len(shards), top_value / len(shards))
        level = level * jnp.repeat(jnp.exp(heights), shape[position] // shards_of).reshape((-1,) + (1,) * (len(shape) - 1 - position))
    return level


def split_up(count, total, bound, lean):
    portions = [(1 << 20) // math.isqrt(standing ** lean) + 1 for standing in range(2, count + 1)]
    rest, given = total - bound - (count - 1), [1] * (count - 1)
    while rest > 0:
        free = [i for i in range(count - 1) if given[i] < bound]
        pool, budget = sum([portions[i] for i in free]), rest
        for i in free:
            addition = min(bound - given[i], max(1, budget * portions[i] // pool), rest)
            given[i] = given[i] + addition
            rest = rest - addition
    return np.array([bound] + given)


def ragged(rng, number_of, total, bound, lean):
    if number_of == 2:
        one = jax.random.randint(rng, (), max(1, total - bound), min(bound, total - 1) + 1)
        return jnp.stack([one, total - one])
    sizes = jnp.asarray(split_up(number_of, total, bound, lean), jnp.int32)
    couples = (number_of - 1) // 2
    giver, receiver = sizes[1:1 + 2 * couples:2], sizes[2:2 + 2 * couples:2]
    room = jnp.minimum(giver - 1, bound - receiver)
    moved = jax.random.randint(jax.random.fold_in(rng, 1), (couples,), 0, 1 << 20) % (room + 1)
    sizes = sizes.at[1:1 + 2 * couples:2].set(giver - moved).at[2:2 + 2 * couples:2].set(receiver + moved)
    return sizes[jax.random.permutation(jax.random.fold_in(rng, 2), number_of)]


def centred(stream_key, dims, width, limit, cuts=(), held_as=jnp.bfloat16):
    array = jax.random.normal(stream_key, dims, jnp.float32) * width
    if len(cuts) > 0:
        array = shard_levels(stream_key, dims, cuts, -0.22, 0.18) * array
    return jnp.clip(array, min=-limit, max=limit).astype(held_as)


def setup_inputs(seed: int = 0) -> dict:
    splits = jax.random.split(jax.random.key(seed), 8)
    return {
        "hidden": centred(splits[0], (TOKENS, D), 1.0, 6.0, ((0, 8), (1, 4))),
        "queries": draw_queries(jax.random.fold_in(splits[7], 71), 0),
        "keys_values": draw_keys_values(jax.random.fold_in(splits[7], 71), 0),
        "w_router": centred(splits[3], (D,), D ** -0.5, 0.0625, ((0, 4),)),
        "routed": draw_routed(jax.random.fold_in(splits[7], 71), 0),
        "counts": ragged(splits[5], SHARDS, SHARDS * SLOT_LIMIT * 5 // 8, SLOT_LIMIT, 2).astype(jnp.int32),
        "grad_out": centred(splits[6], (ROUTED, QUERY_HEADS * HEAD_WIDTH), 1.0, 6.0, ((0, 8), (1, 4))),
    }


def reference(hidden, queries, keys_values, w_router, routed, counts, grad_out):
    group = QUERY_HEADS // HK
    logit_scale_factor = 1.0 / math.sqrt(HEAD_WIDTH)
    offsets = (jnp.arange(SHARDS, dtype=jnp.int32) * TOK_DEV)[:, None]
    positions = (routed.astype(jnp.int32) + offsets).reshape(-1)
    live_slots = (jnp.arange(SLOT_LIMIT, dtype=jnp.int32)[None, :] < counts[:, None]).reshape(-1)
    chosen_x = hidden[positions]
    logit = jnp.dot(chosen_x, w_router, preferred_element_type=jnp.float32)
    gate = jax.nn.sigmoid(logit)
    live_float = live_slots.astype(jnp.float32)
    weight_all = gate * live_float
    query_all = queries[positions].reshape(ROUTED, HK, group, HEAD_WIDTH).astype(jnp.float32)
    every_key = keys_values[0][positions].reshape(ROUTED, HK, HEAD_WIDTH).astype(jnp.float32)
    every_value = keys_values[1][positions].reshape(ROUTED, HK, HEAD_WIDTH).astype(jnp.float32)
    upstream_all = grad_out.astype(jnp.float32).reshape(ROUTED, HK, group, HEAD_WIDTH)
    slot_ids = jnp.arange(ROUTED, dtype=jnp.int32)

    def shard_step(carried, shard):
        key_gradient, value_gradient, router_acc = carried
        first_row = shard * SLOT_LIMIT
        routed_query_rows = lax.dynamic_slice_in_dim(query_all, first_row, SLOT_LIMIT, 0)
        upstream = lax.dynamic_slice_in_dim(upstream_all, first_row, SLOT_LIMIT, 0)
        weight_rows = lax.dynamic_slice_in_dim(weight_all, first_row, SLOT_LIMIT, 0)
        gate_rows = lax.dynamic_slice_in_dim(gate, first_row, SLOT_LIMIT, 0)
        live_rows = lax.dynamic_slice_in_dim(live_float, first_row, SLOT_LIMIT, 0)
        x_rows = lax.dynamic_slice_in_dim(chosen_x, first_row, SLOT_LIMIT, 0)
        query_slots = first_row + jnp.arange(SLOT_LIMIT, dtype=jnp.int32)
        allowed = (slot_ids[None, :] <= query_slots[:, None]) & live_slots[None, :]
        score_matrix = jnp.einsum('vemc,uec->emvu', routed_query_rows, every_key) * logit_scale_factor
        masked = jnp.where(allowed, score_matrix, -jnp.inf)
        row_max = lax.optimization_barrier(jnp.max(masked, axis=-1))
        lse = row_max + jnp.log(lax.optimization_barrier(jnp.sum(jnp.exp(masked - row_max[..., None]), axis=-1)))
        probs = jnp.exp(masked - lse[..., None])
        probs_narrow = lax.optimization_barrier(probs.astype(jnp.bfloat16)).astype(jnp.float32)
        attention_output = jnp.einsum('psot,tpn->opsn', probs_narrow, every_value)
        out_rows = (attention_output * weight_rows[:, None, None, None]).reshape(SLOT_LIMIT, QUERY_HEADS * HEAD_WIDTH).astype(jnp.bfloat16)
        gradient_rows = lax.optimization_barrier((upstream * weight_rows[:, None, None, None]).astype(jnp.bfloat16)).astype(jnp.float32)
        dlogit = lax.optimization_barrier(jnp.sum(upstream * attention_output, axis=(1, 2, 3))) * gate_rows * (1.0 - gate_rows) * live_rows
        delta = lax.optimization_barrier(jnp.sum(gradient_rows * attention_output, axis=-1)).transpose(1, 2, 0)
        prob_gradient = jnp.einsum('vemc,uec->emvu', gradient_rows, every_value)
        score_gradient = lax.optimization_barrier((probs * (prob_gradient - delta[..., None])).astype(jnp.bfloat16)).astype(jnp.float32)
        query_gradient = (jnp.einsum('psot,tpn->opsn', score_gradient, every_key) * logit_scale_factor).reshape(SLOT_LIMIT, QUERY_HEADS * HEAD_WIDTH).astype(jnp.bfloat16)
        key_gradient = key_gradient + jnp.einsum('cfym,ycfh->mch', score_gradient, routed_query_rows) * logit_scale_factor
        value_gradient = value_gradient + jnp.einsum('cfym,ycfh->mch', probs_narrow, gradient_rows)
        router_acc = router_acc + jnp.dot(dlogit, x_rows.astype(jnp.float32))
        return ((key_gradient, value_gradient, router_acc), (out_rows, query_gradient))
    start_carry = (jnp.zeros((ROUTED, HK, HEAD_WIDTH), jnp.float32), jnp.zeros((ROUTED, HK, HEAD_WIDTH), jnp.float32), jnp.zeros((D,), jnp.float32))
    final, stacked = lax.scan(shard_step, start_carry, jnp.arange(SHARDS, dtype=jnp.int32))
    key_gradient, value_gradient, router_acc = final
    branch_out = stacked[0].reshape(ROUTED, QUERY_HEADS * HEAD_WIDTH)
    grad_queries = stacked[1].reshape(ROUTED, QUERY_HEADS * HEAD_WIDTH)
    grad_keys_values = jnp.stack([key_gradient.reshape(ROUTED, HK * HEAD_WIDTH), value_gradient.reshape(ROUTED, HK * HEAD_WIDTH)]).astype(jnp.bfloat16)
    return (branch_out, grad_queries, grad_keys_values, router_acc)
```

```python
import functools
import math

import jax
import jax.numpy as jnp
from jax import lax
from jax.experimental import pallas as pl
from jax.experimental.pallas import tpu as pltpu
from jax.sharding import PartitionSpec as P

HEAD_WIDTH = 128
LANES = 128
LOG2E = math.log2(math.e)
FAR = 1 << 30
BF16 = jnp.bfloat16
F32 = jnp.float32


def dot(a, b):
    return lax.dot_general(a, b, (((1,), (0,)), ((), ())), preferred_element_type=F32)


def eye(shape):
    return lax.broadcasted_iota(jnp.int32, shape, 0) == lax.broadcasted_iota(jnp.int32, shape, 1)


def row_to_column(row, rows):
    spread = jnp.broadcast_to(row, (rows, row.shape[1]))
    return jnp.sum(jnp.where(eye(spread.shape), spread, 0.0), axis=1, keepdims=True)


def column_to_row(column, width):
    spread = jnp.broadcast_to(column, (column.shape[0], width))
    return jnp.sum(jnp.where(eye(spread.shape), spread, 0.0), axis=0, keepdims=True)


def one_hot(routed_row, tokens):
    slots = routed_row.shape[1]
    column = row_to_column(routed_row.astype(F32), slots).astype(jnp.int32)
    ids = lax.broadcasted_iota(jnp.int32, (slots, tokens), 1)
    return jnp.where(ids == column, 1.0, 0.0).astype(BF16)


def gather_pairs(keys_values, routed, core, split):
    _, tokens, width = keys_values.shape
    slots = routed.shape[1]
    out = jax.ShapeDtypeStruct((2, slots, HEAD_WIDTH), BF16)

    def body(core_ref, routed_ref, kv_ref, *outs):
        select = outs[-1]

        @pl.when(pl.program_id(0) == 0)
        def _():
            select[...] = one_hot(routed_ref[...], tokens)

        rows = dot(select[...], kv_ref[0]).astype(BF16)
        if split == 1:
            outs[0][0] = rows
        else:
            first = core_ref[0] == 0
            low, high = rows[:, :HEAD_WIDTH], rows[:, HEAD_WIDTH:]
            outs[0][0] = jnp.where(first, low, high)
            outs[1][0] = jnp.where(first, high, low)

    return pl.pallas_call(
        body,
        grid_spec=pltpu.PrefetchScalarGridSpec(
            num_scalar_prefetch=1,
            grid=(2,),
            in_specs=[
                pl.BlockSpec((1, slots), lambda i, c: (0, 0)),
                pl.BlockSpec((1, tokens, width), lambda i, c: (i, 0, 0)),
            ],
            out_specs=[pl.BlockSpec((1, slots, HEAD_WIDTH), lambda i, c: (i, 0, 0))] * split,
            scratch_shapes=[pltpu.VMEM((slots, tokens), BF16)],
        ),
        out_shape=[out] * split,
        name="gather_pairs",
    )(core, routed, keys_values)


def gather_rows(queries, hidden, w_router, routed, grad_out, core, split, wide):
    tokens, width = queries.shape
    slots = routed.shape[1]
    half = width // split
    step = 256
    steps = width // step
    per_half = half // step

    def body(core_ref, routed_ref, q_ref, x_ref, w_ref, g_ref, *refs):
        outs, (x_out, logit_ref, select, acc) = refs[:split], refs[split:]
        j = pl.program_id(0)

        @pl.when(j == 0)
        def _():
            select[...] = one_hot(routed_ref[...], tokens)
            acc[...] = jnp.zeros_like(acc)

        q_rows = dot(select[...], q_ref[...]).astype(BF16)
        at = pl.ds(pl.multiple_of((j % per_half) * step, step), step)
        if split == 1:
            outs[0][0, :, at] = q_rows
            outs[0][1, :, at] = g_ref[...]
        else:
            mine = j // per_half == core_ref[0]

            @pl.when(mine)
            def _():
                outs[0][0, :, at] = q_rows
                outs[0][1, :, at] = g_ref[...]

            @pl.when(jnp.logical_not(mine))
            def _():
                outs[1][0, :, at] = q_rows
                outs[1][1, :, at] = g_ref[...]

        x_rows = dot(select[...], x_ref[...])
        x_out[...] = x_rows.astype(BF16)
        product = x_rows * w_ref[...].astype(F32)
        for t in range(step // LANES):
            acc[...] += product[:, t * LANES : (t + 1) * LANES]

        @pl.when(j == steps - 1)
        def _():
            logit_ref[...] = column_to_row(jnp.sum(acc[...], axis=1, keepdims=True), wide)

    pair = jax.ShapeDtypeStruct((2, slots, half), BF16)
    return pl.pallas_call(
        body,
        grid_spec=pltpu.PrefetchScalarGridSpec(
            num_scalar_prefetch=1,
            grid=(steps,),
            in_specs=[
                pl.BlockSpec((1, slots), lambda j, c: (0, 0)),
                pl.BlockSpec((tokens, step), lambda j, c: (0, j)),
                pl.BlockSpec((tokens, step), lambda j, c: (0, j)),
                pl.BlockSpec((1, step), lambda j, c: (0, j)),
                pl.BlockSpec((slots, step), lambda j, c: (0, j)),
            ],
            out_specs=[pl.BlockSpec((2, slots, half), lambda j, c: (0, 0, 0))] * split
            + [
                pl.BlockSpec((slots, step), lambda j, c: (0, j)),
                pl.BlockSpec((1, wide), lambda j, c: (0, 0)),
            ],
            scratch_shapes=[pltpu.VMEM((slots, tokens), BF16), pltpu.VMEM((slots, LANES), F32)],
        ),
        out_shape=[pair] * split
        + [
            jax.ShapeDtypeStruct((slots, width), BF16),
            jax.ShapeDtypeStruct((1, wide), F32),
        ],
        name="gather_rows",
    )(core, routed, queries, hidden, w_router.reshape(1, width), grad_out)


class Plan:
    def __init__(self, seq, split, slots, group, wide):
        self.seq, self.split, self.slots, self.group, self.wide = seq, split, slots, group, wide
        self.tile = 256
        self.keys = -(-seq * slots // self.tile) * self.tile
        self.rows = 32
        self.chunks = slots // self.rows
        self.lanes = self.rows * group


def round_up(count, unit):
    return ((count + (unit - 1)) // unit) * unit


def offset_of(counts_ref, shard, seq):
    def add(j, total):
        return total + jnp.where(j < shard, round_up(counts_ref[j], 16), 0)

    return lax.fori_loop(0, seq, add, jnp.int32(0), unroll=True)


def stack_heads(block, plan):
    return jnp.concatenate(
        [block[:, h * HEAD_WIDTH : (h + 1) * HEAD_WIDTH] for h in range(plan.group)], axis=0
    )


def weights_to_columns(logit_row, live, columns, plan):
    gate = 1.0 / (1.0 + jnp.exp(-logit_row))
    slot = lax.broadcasted_iota(jnp.int32, gate.shape, 1)
    weight = jnp.where(slot < live, gate, 0.0)
    for b in range(plan.wide // LANES):
        column = row_to_column(weight[:, b * LANES : (b + 1) * LANES], LANES)
        columns[b * LANES : (b + 1) * LANES, :] = jnp.broadcast_to(column, (LANES, LANES))


def query_positions(offset, chunk, plan):
    lane = lax.broadcasted_iota(jnp.int32, (1, plan.lanes), 1)
    return offset + chunk * plan.rows + lane % plan.rows


def whole(shape):
    return pl.BlockSpec(shape, lambda *_: (0,) * len(shape))


def attend(plan, shard, counts, pairs, sides, logits):
    seq, split, slots, tile, lanes = plan.seq, plan.split, plan.slots, plan.tile, plan.lanes
    scale = LOG2E / math.sqrt(HEAD_WIDTH)
    reps = lanes // LANES

    def body(shard_ref, counts_ref, *refs):
        refs = list(refs)
        pair_refs = [refs.pop(0) for _ in range(seq)]
        side_refs = [refs.pop(0) for _ in range(split)]
        logit_refs = [refs.pop(0) for _ in range(split)]
        out_refs = [refs.pop(0) for _ in range(split)]
        gate_refs = [refs.pop(0) for _ in range(split)]
        keys, values, place, lse_ref, delta_ref, values_t, scores, columns, gate_column = refs
        own = shard_ref[0]
        keys[...] = jnp.zeros_like(keys)
        values[...] = jnp.zeros_like(values)
        place[...] = jnp.full(place.shape, FAR, jnp.int32)
        for i in range(seq):
            source = own ^ i
            live = counts_ref[source]
            start = offset_of(counts_ref, source, seq)

            def move(t, _, i=i, live=live, start=start):
                at = pl.multiple_of(t * 16, 16)
                to = pl.multiple_of(start + t * 16, 16)
                keys[pl.ds(to, 16), :] = pair_refs[i][0, pl.ds(at, 16), :]
                values[pl.ds(to, 16), :] = pair_refs[i][1, pl.ds(at, 16), :]
                slot = at + lax.broadcasted_iota(jnp.int32, (16, LANES), 0)
                place[pl.ds(to, 16), :] = jnp.where(slot < live, start + slot, FAR)
                return 0

            lax.fori_loop(0, (live + 15) // 16, move, 0)
        values_t[...] = values[...].T
        for side in range(split):
            mine = own ^ side
            live = counts_ref[mine]
            offset = offset_of(counts_ref, mine, seq)
            weights_to_columns(logit_refs[side][...], live, columns, plan)
            out_refs[side][...] = jnp.zeros_like(out_refs[side])
            gate_column[...] = jnp.zeros_like(gate_column)

            def chunk_step(chunk, _, side=side, live=live, offset=offset):
                first = pl.multiple_of(chunk * plan.rows, plan.rows)
                at = pl.ds(first, plan.rows)
                q_t = stack_heads(side_refs[side][0, at, :], plan).T
                upstream = stack_heads(side_refs[side][1, at, :], plan).astype(F32)
                weight = columns[at, :]
                weight_all = jnp.concatenate([weight] * plan.group, axis=0)
                positions = query_positions(offset, chunk, plan)
                tiles = (offset + jnp.minimum(live, first + plan.rows) + tile - 1) // tile

                def score(t, running):
                    here = pl.ds(pl.multiple_of(t * tile, tile), tile)
                    s = dot(keys[here, :], q_t) * scale
                    where = place[here, :]
                    allowed = jnp.concatenate([where] * reps, axis=1) <= positions
                    s = jnp.where(allowed, s, -jnp.inf)
                    scores[here, :] = s
                    return jnp.maximum(running, jnp.max(s, axis=0, keepdims=True))

                top = lax.fori_loop(0, tiles, score, jnp.full((1, lanes), -1e30, F32))

                def total(t, carried):
                    summed, out_t = carried
                    here = pl.ds(pl.multiple_of(t * tile, tile), tile)
                    p = jnp.exp2(scores[here, :] - top)
                    summed = summed + jnp.sum(p, axis=0, keepdims=True)
                    return (summed, out_t + dot(values_t[:, here], p.astype(BF16)))

                summed, out_t = lax.fori_loop(
                    0,
                    tiles,
                    total,
                    (jnp.zeros((1, lanes), F32), jnp.zeros((HEAD_WIDTH, lanes), F32)),
                )
                out_t = out_t * (1.0 / summed)
                index = side * plan.chunks + chunk
                lse_ref[pl.ds(index, 1)] = (top + jnp.log2(summed))[None]
                out = out_t.T
                narrow = (upstream * weight_all).astype(BF16).astype(F32)
                delta_ref[pl.ds(index, 1)] = jnp.sum(narrow.T * out_t, axis=0, keepdims=True)[None]
                raw = upstream * out
                gate = raw[: plan.rows]
                for h in range(1, plan.group):
                    gate = gate + raw[h * plan.rows : (h + 1) * plan.rows]
                gate_column[at, :] = gate
                weighted = (out * weight_all).astype(BF16)
                for h in range(plan.group):
                    out_refs[side][at, h * HEAD_WIDTH : (h + 1) * HEAD_WIDTH] = weighted[
                        h * plan.rows : (h + 1) * plan.rows
                    ]
                return 0

            lax.fori_loop(0, (live + plan.rows - 1) // plan.rows, chunk_step, 0)
            gate_refs[side][...] = column_to_row(
                jnp.sum(gate_column[...], axis=1, keepdims=True), plan.wide
            )

    width = plan.group * HEAD_WIDTH
    pair = (2, slots, HEAD_WIDTH)
    stats = (split * plan.chunks, 1, lanes)
    shapes = (
        [jax.ShapeDtypeStruct((slots, width), BF16)] * split
        + [jax.ShapeDtypeStruct((1, plan.wide), F32)] * split
        + [
            jax.ShapeDtypeStruct((plan.keys, HEAD_WIDTH), BF16),
            jax.ShapeDtypeStruct((plan.keys, HEAD_WIDTH), BF16),
            jax.ShapeDtypeStruct((plan.keys, LANES), jnp.int32),
            jax.ShapeDtypeStruct(stats, F32),
            jax.ShapeDtypeStruct(stats, F32),
        ]
    )
    return pl.pallas_call(
        body,
        grid_spec=pltpu.PrefetchScalarGridSpec(
            num_scalar_prefetch=2,
            grid=(1,),
            in_specs=[whole(pair)] * seq
            + [whole((2, slots, width))] * split
            + [whole((1, plan.wide))] * split,
            out_specs=[whole(s.shape) for s in shapes],
            scratch_shapes=[
                pltpu.VMEM((HEAD_WIDTH, plan.keys), BF16),
                pltpu.VMEM((plan.keys, lanes), F32),
                pltpu.VMEM((plan.wide, LANES), F32),
                pltpu.VMEM((slots, LANES), F32),
            ],
        ),
        out_shape=shapes,
        name="attend",
    )(shard, counts, *pairs, *sides, *logits)


def attend_back(plan, shard, counts, keys, values, place, lse, delta, sides, logits):
    seq, split, slots, tile, lanes = plan.seq, plan.split, plan.slots, plan.tile, plan.lanes
    inverse = 1.0 / math.sqrt(HEAD_WIDTH)
    scale = LOG2E * inverse
    reps = lanes // LANES

    def body(shard_ref, counts_ref, keys, values, place, lse_ref, delta_ref, *refs):
        refs = list(refs)
        side_refs = [refs.pop(0) for _ in range(split)]
        logit_refs = [refs.pop(0) for _ in range(split)]
        out_refs = [refs.pop(0) for _ in range(split)]
        pair_refs = [refs.pop(0) for _ in range(seq)]
        keys_t, key_acc, value_acc, columns = refs
        own = shard_ref[0]
        keys_t[...] = keys[...].T
        key_acc[...] = jnp.zeros_like(key_acc)
        value_acc[...] = jnp.zeros_like(value_acc)
        for side in range(split):
            mine = own ^ side
            live = counts_ref[mine]
            offset = offset_of(counts_ref, mine, seq)
            weights_to_columns(logit_refs[side][...], live, columns, plan)
            out_refs[side][...] = jnp.zeros_like(out_refs[side])

            def chunk_step(chunk, _, side=side, live=live, offset=offset):
                first = pl.multiple_of(chunk * plan.rows, plan.rows)
                at = pl.ds(first, plan.rows)
                q = stack_heads(side_refs[side][0, at, :], plan)
                upstream = stack_heads(side_refs[side][1, at, :], plan).astype(F32)
                weight_all = jnp.concatenate([columns[at, :]] * plan.group, axis=0)
                narrow = (upstream * weight_all).astype(BF16)
                q_t = q.T
                narrow_t = narrow.T
                positions = query_positions(offset, chunk, plan)
                index = side * plan.chunks + chunk
                lse_row = lse_ref[pl.ds(index, 1)][0]
                delta_row = delta_ref[pl.ds(index, 1)][0]
                tiles = (offset + jnp.minimum(live, first + plan.rows) + tile - 1) // tile

                def back(t, grad_t):
                    here = pl.ds(pl.multiple_of(t * tile, tile), tile)
                    s = dot(keys[here, :], q_t) * scale
                    where = place[here, :]
                    allowed = jnp.concatenate([where] * reps, axis=1) <= positions
                    p = jnp.where(allowed, jnp.exp2(s - lse_row), 0.0)
                    value_acc[here, :] += dot(p.astype(BF16), narrow)
                    dp = dot(values[here, :], narrow_t)
                    ds = (p * (dp - delta_row)).astype(BF16)
                    key_acc[here, :] += dot(ds, q)
                    return grad_t + dot(keys_t[:, here], ds)

                grad_t = lax.fori_loop(0, tiles, back, jnp.zeros((HEAD_WIDTH, lanes), F32))
                grad = (grad_t.T * inverse).astype(BF16)
                for h in range(plan.group):
                    out_refs[side][at, h * HEAD_WIDTH : (h + 1) * HEAD_WIDTH] = grad[
                        h * plan.rows : (h + 1) * plan.rows
                    ]
                return 0

            lax.fori_loop(0, (live + plan.rows - 1) // plan.rows, chunk_step, 0)
        for i in range(seq):
            source = own ^ i
            live = counts_ref[source]
            start = offset_of(counts_ref, source, seq)
            pair_refs[i][...] = jnp.zeros_like(pair_refs[i])

            def move(t, _, i=i, start=start):
                at = pl.multiple_of(t * 16, 16)
                here = pl.ds(pl.multiple_of(start + t * 16, 16), 16)
                pair_refs[i][0, pl.ds(at, 16), :] = (key_acc[here, :] * inverse).astype(BF16)
                pair_refs[i][1, pl.ds(at, 16), :] = value_acc[here, :].astype(BF16)
                return 0

            lax.fori_loop(0, (live + 15) // 16, move, 0)

    width = plan.group * HEAD_WIDTH
    pair = (2, slots, HEAD_WIDTH)
    shapes = [jax.ShapeDtypeStruct((slots, width), BF16)] * split + [
        jax.ShapeDtypeStruct(pair, BF16)
    ] * seq
    return pl.pallas_call(
        body,
        grid_spec=pltpu.PrefetchScalarGridSpec(
            num_scalar_prefetch=2,
            grid=(1,),
            in_specs=[whole(a.shape) for a in (keys, values, place, lse, delta)]
            + [whole((2, slots, width))] * split
            + [whole((1, plan.wide))] * split,
            out_specs=[whole(s.shape) for s in shapes],
            scratch_shapes=[
                pltpu.VMEM((HEAD_WIDTH, plan.keys), BF16),
                pltpu.VMEM((plan.keys, HEAD_WIDTH), F32),
                pltpu.VMEM((plan.keys, HEAD_WIDTH), F32),
                pltpu.VMEM((plan.wide, LANES), F32),
            ],
        ),
        out_shape=shapes,
        name="attend_back",
    )(shard, counts, keys, values, place, lse, delta, *sides, *logits)


def router_part(shard, counts, logit, gates, rows, wide):
    slots, width = rows.shape

    def body(shard_ref, counts_ref, logit_ref, *refs):
        gate_refs, rows_ref, out_ref = refs[:-2], refs[-2], refs[-1]
        term = gate_refs[0][...]
        for ref in gate_refs[1:]:
            term = term + ref[...]
        gate = 1.0 / (1.0 + jnp.exp(-logit_ref[...]))
        slot = lax.broadcasted_iota(jnp.int32, gate.shape, 1)
        dlogit = jnp.where(slot < counts_ref[shard_ref[0]], term * gate * (1.0 - gate), 0.0)
        column = row_to_column(dlogit, slots)
        for b in range(width // LANES):
            at = slice(b * LANES, (b + 1) * LANES)
            out_ref[:, at] = jnp.sum(
                rows_ref[:, at].astype(F32) * column, axis=0, keepdims=True
            )

    return pl.pallas_call(
        body,
        grid_spec=pltpu.PrefetchScalarGridSpec(
            num_scalar_prefetch=2,
            grid=(1,),
            in_specs=[whole((1, wide))] * (1 + len(gates)) + [whole(rows.shape)],
            out_specs=whole((1, width)),
        ),
        out_shape=jax.ShapeDtypeStruct((1, width), F32),
        name="router_part",
    )(shard, counts, logit, *gates, rows)


def join_halves(core, mine, taken):
    slots, half = mine[0].shape
    number = len(mine)

    def body(core_ref, *refs):
        outs = refs[2 * number :]
        for a in range(number):
            @pl.when(pl.program_id(0) == 0)
            def _(a=a):
                outs[a][...] = refs[a][...]

            @pl.when(pl.program_id(0) == 1)
            def _(a=a):
                outs[a][...] = refs[number + a][...]

    return pl.pallas_call(
        body,
        grid_spec=pltpu.PrefetchScalarGridSpec(
            num_scalar_prefetch=1,
            grid=(2,),
            in_specs=[whole((slots, half))] * (2 * number),
            out_specs=[pl.BlockSpec((slots, half), lambda i, c: (0, i ^ c[0]))] * number,
        ),
        out_shape=[jax.ShapeDtypeStruct((slots, 2 * half), BF16)] * number,
        name="join_halves",
    )(core, *mine, *taken)


def finish(core, pairs, split, routers):
    _, slots, head = pairs[0].shape
    width = routers[0].shape[1]
    number = len(pairs)

    def body(core_ref, *refs):
        pair_refs, router_refs = refs[:number], refs[number:-2]
        out_ref, router_out = refs[-2], refs[-1]
        total = router_refs[0][...]
        for ref in router_refs[1:]:
            total = total + ref[...]
        router_out[...] = total
        sums = []
        for side in range(split):
            acc = pair_refs[side][...].astype(F32)
            for i in range(side + split, number, split):
                acc = acc + pair_refs[i][...].astype(F32)
            sums.append(acc.astype(BF16))
        if split == 1:
            out_ref[...] = sums[0]
        else:
            first = core_ref[0] == 0
            out_ref[:, :, :head] = jnp.where(first, sums[0], sums[1])
            out_ref[:, :, head:] = jnp.where(first, sums[1], sums[0])

    return pl.pallas_call(
        body,
        grid_spec=pltpu.PrefetchScalarGridSpec(
            num_scalar_prefetch=1,
            grid=(1,),
            in_specs=[whole(pairs[0].shape)] * number + [whole((1, width))] * len(routers),
            out_specs=[whole((2, slots, split * head)), whole((1, width))],
        ),
        out_shape=[
            jax.ShapeDtypeStruct((2, slots, split * head), BF16),
            jax.ShapeDtypeStruct((1, width), F32),
        ],
        name="finish",
    )(core, *pairs, *routers)


def shards(hidden, queries, keys_values, w_router, routed, counts, grad_out):
    seq = lax.axis_size("seq")
    tp = lax.axis_size("tp")
    slots = routed.shape[1]
    kv_local = keys_values.shape[2] // HEAD_WIDTH
    q_local = queries.shape[1] // HEAD_WIDTH
    group = q_local // kv_local
    split = 2 if kv_local == 2 else 1
    wide = -(-slots // LANES) * LANES
    if kv_local != split or seq & (seq - 1) or slots % 32 or group * 32 % LANES:
        raise ValueError("unsupported sizes")
    plan = Plan(seq, split, slots, group, wide)
    own = lax.axis_index("seq").astype(jnp.int32)
    shard = own.reshape(1)
    core = (own % 2).reshape(1)

    def across(value, k):
        return lax.ppermute(value, "seq", [(i, i ^ k) for i in range(seq)])

    def around(value, k):
        return lax.ppermute(value, "tp", [(i, (i + k) % tp) for i in range(tp)])

    sent = gather_pairs(keys_values, routed, core, split)
    pairs = [sent[0]] + [across(sent[k % split], k) for k in range(1, seq)]
    *parts, chosen_x, logit_part = gather_rows(
        queries, hidden, w_router, routed, grad_out, core, split, wide
    )
    sides = [parts[0]] + [across(part, 1) for part in parts[1:]]
    logit = logit_part
    for k in range(1, tp):
        logit = logit + around(logit_part, k)
    logits = [logit] + [across(logit, 1)] * (split - 1)

    results = attend(plan, shard, counts, pairs, sides, logits)
    branches, gates = results[:split], results[split : 2 * split]
    keys, values, place, lse, delta = results[2 * split :]
    gate = gates[0]
    for part in gates[1:]:
        gate = gate + across(part, 1)
    gate_terms = [gate] + [around(gate, k) for k in range(1, tp)]

    results = attend_back(plan, shard, counts, keys, values, place, lse, delta, sides, logits)
    grads, backs = results[:split], results[split:]
    arrived = [backs[0]] + [across(backs[k], k) for k in range(1, seq)]
    router = router_part(shard, counts, logit, gate_terms, chosen_x, wide)
    router = router + across(router, 1)
    routers = [router] + [across(router, k) for k in range(2, seq, 2)]
    if split == 1:
        branch_out, grad_queries = branches[0], grads[0]
    else:
        branch_out, grad_queries = join_halves(
            core, [branches[0], grads[0]], [across(branches[1], 1), across(grads[1], 1)]
        )
    grad_keys_values, grad_router = finish(core, arrived, split, routers)
    return (branch_out, grad_queries, grad_keys_values, grad_router.reshape(-1))


def solution(mesh):
    in_specs = (
        P("seq", "tp"),
        P("seq", "tp"),
        P(None, "seq", "tp"),
        P("tp"),
        P("seq", None),
        P(),
        P("seq", "tp"),
    )
    out_specs = (P("seq", "tp"), P("seq", "tp"), P(None, "seq", "tp"), P("tp"))
    return jax.shard_map(shards, mesh=mesh, in_specs=in_specs, out_specs=out_specs, check_vma=False)
```

```python
import functools
import math

import jax
import jax.numpy as jnp
from jax import lax
from jax.experimental import pallas as pl
from jax.experimental.pallas import tpu as pltpu
from jax.sharding import PartitionSpec as P


HEAD_WIDTH = 128
LANES = 128
LOG2E = math.log2(math.e)
FAR = 1 << 30
BF16 = jnp.bfloat16
F32 = jnp.float32


def dot(a, b):
    return lax.dot_general(a, b, (((1,), (0,)), ((), ())), preferred_element_type=F32)


def eye(shape):
    return lax.broadcasted_iota(jnp.int32, shape, 0) == lax.broadcasted_iota(jnp.int32, shape, 1)


def row_to_column(row, rows):
    spread = jnp.broadcast_to(row, (rows, row.shape[1]))
    return jnp.sum(jnp.where(eye(spread.shape), spread, 0.0), axis=1, keepdims=True)


def column_to_row(column, width):
    spread = jnp.broadcast_to(column, (column.shape[0], width))
    return jnp.sum(jnp.where(eye(spread.shape), spread, 0.0), axis=0, keepdims=True)


def one_hot(routed_row, tokens):
    slots = routed_row.shape[1]
    column = row_to_column(routed_row.astype(F32), slots).astype(jnp.int32)
    ids = lax.broadcasted_iota(jnp.int32, (slots, tokens), 1)
    return jnp.where(ids == column, 1.0, 0.0).astype(BF16)


def rows_of(split, core, rows):
    if split == 1:
        return [rows]
    low, high = rows[:, :HEAD_WIDTH], rows[:, HEAD_WIDTH:]
    first = core == 0
    return [jnp.where(first, low, high), jnp.where(first, high, low)]


def pieces(rows, number=5):
    size = -(-rows // number // 16) * 16
    return [(at, min(size, rows - at)) for at in range(0, rows, size)]


def gather_first(keys_values, hidden, w_router, routed, core, split, wide):
    _, tokens, width = keys_values.shape
    model = hidden.shape[1]
    slots = routed.shape[1]
    step = 256
    parts = pieces(tokens)

    def body(core_ref, routed_ref, w_ref, kv_hbm, x_hbm, *refs):
        outs, (x_out, logit_ref, kv_buf, x_buf, acc, kv_sem, x_sem) = refs[:split], refs[split:]
        kv_copies = [
            pltpu.make_async_copy(kv_hbm.at[i], kv_buf.at[i], kv_sem.at[i]) for i in range(2)
        ]
        x_copies = [
            pltpu.make_async_copy(
                x_hbm.at[pl.ds(at, size)], x_buf.at[pl.ds(at, size)], x_sem.at[p]
            )
            for p, (at, size) in enumerate(parts)
        ]
        for copy in kv_copies + x_copies:
            copy.start()
        select = one_hot(routed_ref[...], tokens)
        for i in range(2):
            kv_copies[i].wait()
            rows = dot(select, kv_buf[i]).astype(BF16)
            for out, part in zip(outs, rows_of(split, core_ref[0], rows)):
                out[i] = part
        for copy in x_copies:
            copy.wait()
        acc[...] = jnp.zeros_like(acc)
        for j in range(model // step):
            rows = dot(select, x_buf[:, j * step : (j + 1) * step])
            x_out[:, j * step : (j + 1) * step] = rows.astype(BF16)
            for t in range(step // LANES):
                b = j * (step // LANES) + t
                weight = w_ref[b : b + 1, :].astype(F32)
                acc[...] += rows[:, t * LANES : (t + 1) * LANES] * weight
        logit_ref[...] = column_to_row(jnp.sum(acc[...], axis=1, keepdims=True), wide)

    return pl.pallas_call(
        body,
        grid_spec=pltpu.PrefetchScalarGridSpec(
            num_scalar_prefetch=1,
            grid=(1,),
            in_specs=[
                whole((1, slots)),
                whole((model // LANES, LANES)),
                pl.BlockSpec(memory_space=pltpu.HBM),
                pl.BlockSpec(memory_space=pltpu.HBM),
            ],
            out_specs=[whole((2, slots, HEAD_WIDTH))] * split
            + [whole((slots, model)), whole((1, wide))],
            scratch_shapes=[
                pltpu.VMEM((2, tokens, width), BF16),
                pltpu.VMEM((tokens, model), BF16),
                pltpu.VMEM((slots, LANES), F32),
                pltpu.SemaphoreType.DMA((2,)),
                pltpu.SemaphoreType.DMA((len(parts),)),
            ],
        ),
        out_shape=[jax.ShapeDtypeStruct((2, slots, HEAD_WIDTH), BF16)] * split
        + [
            jax.ShapeDtypeStruct((slots, model), BF16),
            jax.ShapeDtypeStruct((1, wide), F32),
        ],
        compiler_params=pltpu.CompilerParams(vmem_limit_bytes=58 << 20),
        name="gather_first",
    )(core, routed, w_router.reshape(model // LANES, LANES), keys_values, hidden)


def gather_queries(queries, routed, grad_out, core, split, after):
    tokens, width = queries.shape
    slots = routed.shape[1]
    half = width // split
    step = 256
    parts = pieces(tokens)

    def body(core_ref, routed_ref, g_hbm, q_hbm, *refs):
        refs = refs[len(after) :]
        outs, (g_buf, q_buf, rows_buf, sem, g_sem, out_sem) = refs[:split], refs[split:]
        copies = [
            pltpu.make_async_copy(q_hbm.at[pl.ds(at, size)], q_buf.at[pl.ds(at, size)], sem.at[p])
            for p, (at, size) in enumerate(parts)
        ]
        load = pltpu.make_async_copy(g_hbm, g_buf, g_sem)
        for copy in copies + [load]:
            copy.start()
        select = one_hot(routed_ref[...], tokens)

        def give(source, kind):
            for h in range(split):
                columns = pl.ds(h * half, half)
                for o in range(split):
                    copy = pltpu.make_async_copy(
                        source.at[:, columns], outs[o].at[kind], out_sem.at[kind, h]
                    )
                    if split == 1:
                        copy.start()
                    else:
                        pl.when(core_ref[0] == (h ^ o))(copy.start)

        load.wait()
        give(g_buf, 1)
        for copy in copies:
            copy.wait()
        for j in range(width // step):
            at = slice(j * step, (j + 1) * step)
            rows_buf[:, at] = dot(select, q_buf[:, at]).astype(BF16)
        give(rows_buf, 0)
        for kind in range(2):
            for h in range(split):
                pltpu.make_async_copy(
                    g_buf.at[:, pl.ds(h * half, half)], outs[0].at[kind], out_sem.at[kind, h]
                ).wait()

    return pl.pallas_call(
        body,
        grid_spec=pltpu.PrefetchScalarGridSpec(
            num_scalar_prefetch=1,
            grid=(1,),
            in_specs=[whole((1, slots))]
            + [pl.BlockSpec(memory_space=pltpu.HBM)] * 2
            + [pl.BlockSpec(memory_space=pl.ANY)] * len(after),
            out_specs=[pl.BlockSpec(memory_space=pl.ANY)] * split,
            scratch_shapes=[
                pltpu.VMEM((slots, width), BF16),
                pltpu.VMEM((tokens, width), BF16),
                pltpu.VMEM((slots, width), BF16),
                pltpu.SemaphoreType.DMA((len(parts),)),
                pltpu.SemaphoreType.DMA,
                pltpu.SemaphoreType.DMA((2, split)),
            ],
        ),
        out_shape=[jax.ShapeDtypeStruct((2, slots, half), BF16)] * split,
        compiler_params=pltpu.CompilerParams(vmem_limit_bytes=16 << 20),
        name="gather_queries",
    )(core, routed, grad_out, queries, *after)


class Plan:
    def __init__(self, seq, split, slots, group, wide):
        self.seq, self.split, self.slots, self.group, self.wide = seq, split, slots, group, wide
        self.tile = 256
        self.tiles = -(-seq * slots // self.tile)
        self.keys = self.tiles * self.tile
        self.rows = 32
        self.chunks = slots // self.rows
        self.lanes = self.rows * group
        self.blocks = seq // split


def stack_heads(block, plan):
    return jnp.concatenate(
        [block[:, h * HEAD_WIDTH : (h + 1) * HEAD_WIDTH] for h in range(plan.group)], axis=0
    )


def whole(shape):
    return pl.BlockSpec(shape, lambda *_: (0,) * len(shape))


def total_of(refs, side):
    total = refs[0][side : side + 1, :]
    for ref in refs[1:]:
        total = total + ref[side : side + 1, :]
    return total


def gate_of(logit):
    return 1.0 / (1.0 + jnp.exp(-logit))


def repeat(tiles, step, carried):
    if isinstance(tiles, int):
        for t in range(tiles):
            carried = step(t, carried)
        return carried
    return lax.fori_loop(0, tiles, step, carried)


def attend(plan, shard, counts, blocks, sides, logits):
    seq, split, slots, tile, lanes = plan.seq, plan.split, plan.slots, plan.tile, plan.lanes
    inverse = 1.0 / math.sqrt(HEAD_WIDTH)
    scale = LOG2E * inverse
    reps = lanes // LANES
    width = plan.group * HEAD_WIDTH

    def body(shard_ref, counts_ref, *refs):
        refs = list(refs)
        block_refs = [refs.pop(0) for _ in range(plan.blocks)]
        side_hbm = [refs.pop(0) for _ in range(split)]
        logit_refs = [refs.pop(0) for _ in range(len(logits))]
        out_hbm = [refs.pop(0) for _ in range(split)]
        back_refs = [refs.pop(0) for _ in range(plan.blocks)]
        gate_ref = refs.pop(0)
        (side_buf, out_buf, keys, values, place, keys_t, values_t, scores) = refs[:8]
        (key_acc, value_acc, columns, gate_column, starts, in_sem, out_sem) = refs[8:]
        fetch = [
            pltpu.make_async_copy(side_hbm[i], side_buf.at[i], in_sem.at[i]) for i in range(split)
        ]
        for copy in fetch:
            copy.start()
        own = shard_ref[0]
        end = jnp.int32(0)
        for j in range(seq):
            starts[j] = end
            end = end + ((counts_ref[j] + 15) // 16) * 16
        for b in range(plan.blocks):
            for i in range(split):
                source = own ^ (b * split + i)
                live = counts_ref[source]
                start = starts[source]

                def move(t, _, b=b, i=i, live=live, start=start):
                    at = pl.multiple_of(t * 16, 16)
                    to = pl.multiple_of(start + t * 16, 16)
                    keys[pl.ds(to, 16), :] = block_refs[b][i, 0, pl.ds(at, 16), :]
                    values[pl.ds(to, 16), :] = block_refs[b][i, 1, pl.ds(at, 16), :]
                    slot = at + lax.broadcasted_iota(jnp.int32, (16, LANES), 0)
                    place[pl.ds(to, 16), :] = jnp.where(slot < live, start + slot, FAR)
                    return 0

                lax.fori_loop(0, (live + 15) // 16, move, 0)
        tail = pl.ds(pl.multiple_of(end, 16), tile)
        keys[tail, :] = jnp.zeros((tile, HEAD_WIDTH), BF16)
        values[tail, :] = jnp.zeros((tile, HEAD_WIDTH), BF16)
        place[tail, :] = jnp.full((tile, LANES), FAR, jnp.int32)

        def prepare(t, _):
            here = pl.ds(pl.multiple_of(t * tile, tile), tile)
            keys_t[:, here] = keys[here, :].T
            values_t[:, here] = values[here, :].T
            key_acc[here, :] = jnp.zeros((tile, HEAD_WIDTH), F32)
            value_acc[here, :] = jnp.zeros((tile, HEAD_WIDTH), F32)
            return 0

        lax.fori_loop(0, (end + tile - 1) // tile, prepare, 0)
        gate_column[...] = jnp.zeros_like(gate_column)
        for side in range(split):
            weight = gate_of(total_of(logit_refs, side))
            slot = lax.broadcasted_iota(jnp.int32, weight.shape, 1)
            weight = jnp.where(slot < counts_ref[own ^ side], weight, 0.0)
            for b in range(plan.wide // LANES):
                at = slice(b * LANES, (b + 1) * LANES)
                column = row_to_column(weight[:, at], LANES)
                columns[side, at, :] = jnp.broadcast_to(column, (LANES, LANES))
        for copy in fetch:
            copy.wait()

        def chunk_step(u, _):
            side = u // plan.chunks
            mine = own ^ side
            live = counts_ref[mine]
            offset = starts[mine]
            first = pl.multiple_of((u % plan.chunks) * plan.rows, plan.rows)
            at = pl.ds(first, plan.rows)
            needed = (offset + jnp.minimum(live, first + plan.rows) + tile - 1) // tile
            needed = jnp.where(first < live, needed, 0)

            @pl.when(needed == 0)
            def _():
                out_buf[side, :, at, :] = jnp.zeros((2, plan.rows, width), BF16)

            def work(tiles):
                q = stack_heads(side_buf[side, 0, at, :], plan)
                upstream = stack_heads(side_buf[side, 1, at, :], plan).astype(F32)
                weight = jnp.concatenate([columns[side, at, :]] * plan.group, axis=0)
                narrow = (upstream * weight).astype(BF16)
                q_t = q.T
                narrow_t = narrow.T
                lane = lax.broadcasted_iota(jnp.int32, (1, lanes), 1)
                positions = offset + first + lane % plan.rows

                def here_of(t):
                    if isinstance(t, int):
                        return slice(t * tile, (t + 1) * tile)
                    return pl.ds(pl.multiple_of(t * tile, tile), tile)

                def score(t, running):
                    here = here_of(t)
                    s = dot(keys[here, :], q_t) * scale
                    allowed = jnp.concatenate([place[here, :]] * reps, axis=1) <= positions
                    s = jnp.where(allowed, s, -jnp.inf)
                    scores[here, :] = s
                    return jnp.maximum(running, jnp.max(s, axis=0, keepdims=True))

                top = repeat(tiles, score, jnp.full((1, lanes), -1e30, F32))

                def spread(t, carried):
                    summed, out_t = carried
                    here = here_of(t)
                    p = jnp.exp2(scores[here, :] - top)
                    scores[here, :] = p
                    summed = summed + jnp.sum(p, axis=0, keepdims=True)
                    return (summed, out_t + dot(values_t[:, here], p.astype(BF16)))

                summed, out_t = repeat(
                    tiles,
                    spread,
                    (jnp.zeros((1, lanes), F32), jnp.zeros((HEAD_WIDTH, lanes), F32)),
                )
                share = 1.0 / summed
                out_t = out_t * share
                delta = jnp.sum(narrow_t.astype(F32) * out_t, axis=0, keepdims=True)

                def back(t, grad_t):
                    here = here_of(t)
                    p = scores[here, :] * share
                    dp = dot(values[here, :], narrow_t)
                    value_acc[here, :] += dot(p.astype(BF16), narrow)
                    ds = (p * (dp - delta)).astype(BF16)
                    key_acc[here, :] += dot(ds, q)
                    return grad_t + dot(keys_t[:, here], ds)

                grad_t = repeat(tiles, back, jnp.zeros((HEAD_WIDTH, lanes), F32))
                out = out_t.T
                raw = upstream * out
                gate = raw[: plan.rows]
                for h in range(1, plan.group):
                    gate = gate + raw[h * plan.rows : (h + 1) * plan.rows]
                gate_column[side, at, :] = gate
                weighted = (out * weight).astype(BF16)
                grad = (grad_t * inverse).astype(BF16).T
                for h in range(plan.group):
                    heads = slice(h * HEAD_WIDTH, (h + 1) * HEAD_WIDTH)
                    rows = slice(h * plan.rows, (h + 1) * plan.rows)
                    out_buf[side, 0, at, heads] = weighted[rows]
                    out_buf[side, 1, at, heads] = grad[rows]

            if plan.tiles <= 5:
                for tiles in range(1, plan.tiles + 1):
                    pl.when(needed == tiles)(functools.partial(work, tiles))
            else:
                pl.when(needed > 0)(functools.partial(work, needed))
            return 0

        lax.fori_loop(0, split * plan.chunks, chunk_step, 0)
        push = [
            pltpu.make_async_copy(out_buf.at[i], out_hbm[i], out_sem.at[i]) for i in range(split)
        ]
        for copy in push:
            copy.start()
        for side in range(split):
            gate_ref[side : side + 1, :] = column_to_row(
                jnp.sum(gate_column[side], axis=1, keepdims=True), plan.wide
            )
        for b in range(plan.blocks):
            back_refs[b][...] = jnp.zeros_like(back_refs[b])
            for i in range(split):
                source = own ^ (b * split + i)
                live = counts_ref[source]
                start = starts[source]

                def give(t, _, b=b, i=i, start=start):
                    at = pl.ds(pl.multiple_of(t * 16, 16), 16)
                    here = pl.ds(pl.multiple_of(start + t * 16, 16), 16)
                    back_refs[b][i, 0, at, :] = (key_acc[here, :] * inverse).astype(BF16)
                    back_refs[b][i, 1, at, :] = value_acc[here, :].astype(BF16)
                    return 0

                lax.fori_loop(0, (live + 15) // 16, give, 0)
        for copy in push:
            copy.wait()

    block = (split, 2, slots, HEAD_WIDTH)
    side = (2, slots, width)
    return pl.pallas_call(
        body,
        grid_spec=pltpu.PrefetchScalarGridSpec(
            num_scalar_prefetch=2,
            grid=(1,),
            in_specs=[whole(block)] * plan.blocks
            + [pl.BlockSpec(memory_space=pl.ANY)] * split
            + [whole((split, plan.wide))] * len(logits),
            out_specs=[pl.BlockSpec(memory_space=pl.ANY)] * split
            + [whole(block)] * plan.blocks
            + [whole((split, plan.wide))],
            scratch_shapes=[
                pltpu.VMEM((split,) + side, BF16),
                pltpu.VMEM((split,) + side, BF16),
                pltpu.VMEM((plan.keys + tile, HEAD_WIDTH), BF16),
                pltpu.VMEM((plan.keys + tile, HEAD_WIDTH), BF16),
                pltpu.VMEM((plan.keys + tile, LANES), jnp.int32),
                pltpu.VMEM((HEAD_WIDTH, plan.keys), BF16),
                pltpu.VMEM((HEAD_WIDTH, plan.keys), BF16),
                pltpu.VMEM((plan.keys, lanes), F32),
                pltpu.VMEM((plan.keys, HEAD_WIDTH), F32),
                pltpu.VMEM((plan.keys, HEAD_WIDTH), F32),
                pltpu.VMEM((split, plan.wide, LANES), F32),
                pltpu.VMEM((split, slots, LANES), F32),
                pltpu.SMEM((seq,), jnp.int32),
                pltpu.SemaphoreType.DMA((split,)),
                pltpu.SemaphoreType.DMA((split,)),
            ],
        ),
        out_shape=[jax.ShapeDtypeStruct(side, BF16)] * split
        + [jax.ShapeDtypeStruct(block, BF16)] * plan.blocks
        + [jax.ShapeDtypeStruct((split, plan.wide), F32)],
        compiler_params=pltpu.CompilerParams(
            vmem_limit_bytes=(24 << 20) if plan.tiles <= 5 else (48 << 20)
        ),
        name="attend",
    )(shard, counts, *blocks, *sides, *logits)


def router_part(shard, counts, logits, gates, rows, wide, after):
    slots, width = rows[0].shape
    split = len(rows)
    number = len(logits)

    def body(shard_ref, counts_ref, *refs):
        logit_refs, gate_refs = refs[:number], refs[number : 2 * number]
        row_refs, out_ref = refs[2 * number : 2 * number + split], refs[-1]
        columns = []
        for side in range(split):
            gate = gate_of(total_of(logit_refs, side))
            term = total_of(gate_refs, side)
            slot = lax.broadcasted_iota(jnp.int32, gate.shape, 1)
            live = slot < counts_ref[shard_ref[0] ^ side]
            columns.append(
                jnp.broadcast_to(
                    row_to_column(jnp.where(live, term * gate * (1.0 - gate), 0.0), slots),
                    (slots, LANES),
                )
            )
        for b in range(width // LANES):
            at = slice(b * LANES, (b + 1) * LANES)
            product = row_refs[0][:, at].astype(F32) * columns[0]
            for side in range(1, split):
                product = product + row_refs[side][:, at].astype(F32) * columns[side]
            out_ref[b : b + 1, :] = jnp.sum(product, axis=0, keepdims=True)

    return pl.pallas_call(
        body,
        grid_spec=pltpu.PrefetchScalarGridSpec(
            num_scalar_prefetch=2,
            grid=(1,),
            in_specs=[whole((split, wide))] * (2 * number)
            + [whole((slots, width))] * split
            + [pl.BlockSpec(memory_space=pl.ANY)] * len(after),
            out_specs=whole((width // LANES, LANES)),
        ),
        out_shape=jax.ShapeDtypeStruct((width // LANES, LANES), F32),
        compiler_params=pltpu.CompilerParams(vmem_limit_bytes=16 << 20),
        name="router_part",
    )(shard, counts, *logits, *gates, *rows, *after)


def join_halves(core, mine, taken):
    _, slots, half = mine.shape

    def body(core_ref, mine_ref, taken_ref, *outs):
        for a in range(2):
            @pl.when(pl.program_id(0) == 0)
            def _(a=a):
                outs[a][...] = mine_ref[a]

            @pl.when(pl.program_id(0) == 1)
            def _(a=a):
                outs[a][...] = taken_ref[a]

    return pl.pallas_call(
        body,
        grid_spec=pltpu.PrefetchScalarGridSpec(
            num_scalar_prefetch=1,
            grid=(2,),
            in_specs=[whole((2, slots, half))] * 2,
            out_specs=[pl.BlockSpec((slots, half), lambda i, c: (0, i ^ c[0]))] * 2,
        ),
        out_shape=[jax.ShapeDtypeStruct((slots, 2 * half), BF16)] * 2,
        compiler_params=pltpu.CompilerParams(vmem_limit_bytes=16 << 20),
        name="join_halves",
    )(core, mine, taken)


def add_up(blocks, after):
    split = blocks[0].shape[0]
    number = len(blocks)
    shape = blocks[0].shape[1:]

    def body(*refs):
        ins, outs = refs[:number], refs[number + len(after) :]
        for side in range(split):
            acc = ins[0][side].astype(F32)
            for ref in ins[1:]:
                acc = acc + ref[side].astype(F32)
            outs[side][...] = acc.astype(BF16)

    return pl.pallas_call(
        body,
        grid=(1,),
        in_specs=[whole(blocks[0].shape)] * number
        + [pl.BlockSpec(memory_space=pl.ANY)] * len(after),
        out_specs=[whole(shape)] * split,
        out_shape=[jax.ShapeDtypeStruct(shape, BF16)] * split,
        compiler_params=pltpu.CompilerParams(vmem_limit_bytes=16 << 20),
        name="add_up",
    )(*blocks, *after)


def finish(core, mine, taken, routers):
    _, slots, head = mine.shape
    number = len(routers)

    def body(core_ref, mine_ref, taken_ref, *refs):
        out_ref, router_out = refs[number:]
        first = core_ref[0] == 0
        a, b = mine_ref[...], taken_ref[...]
        out_ref[:, :, :head] = jnp.where(first, a, b)
        out_ref[:, :, head:] = jnp.where(first, b, a)
        total = refs[0][...]
        for ref in refs[1:number]:
            total = total + ref[...]
        router_out[...] = total

    return pl.pallas_call(
        body,
        grid_spec=pltpu.PrefetchScalarGridSpec(
            num_scalar_prefetch=1,
            grid=(1,),
            in_specs=[whole(mine.shape)] * 2 + [whole(routers[0].shape)] * number,
            out_specs=[whole((2, slots, 2 * head)), whole(routers[0].shape)],
        ),
        out_shape=[
            jax.ShapeDtypeStruct((2, slots, 2 * head), BF16),
            jax.ShapeDtypeStruct(routers[0].shape, F32),
        ],
        compiler_params=pltpu.CompilerParams(vmem_limit_bytes=16 << 20),
        name="finish",
    )(core, mine, taken, *routers)


def shards(hidden, queries, keys_values, w_router, routed, counts, grad_out):
    seq = lax.axis_size("seq")
    tp = lax.axis_size("tp")
    slots = routed.shape[1]
    kv_local = keys_values.shape[2] // HEAD_WIDTH
    q_local = queries.shape[1] // HEAD_WIDTH
    group = q_local // kv_local
    split = 2 if kv_local == 2 else 1
    wide = -(-slots // LANES) * LANES
    if kv_local != split or seq & (seq - 1) or slots % 32 or group * 32 % LANES:
        raise ValueError("unsupported sizes")
    plan = Plan(seq, split, slots, group, wide)
    own = lax.axis_index("seq").astype(jnp.int32)
    shard = own.reshape(1)
    core = (own % 2).reshape(1)

    def across(value, k):
        return lax.ppermute(value, "seq", [(i, i ^ k) for i in range(seq)])

    def around(value, k):
        return lax.ppermute(value, "tp", [(i, (i + k) % tp) for i in range(tp)])

    far_first = sorted(range(split, seq, split), key=lambda k: -bin(k).count("1"))

    *sent, chosen_x, logit_part = gather_first(
        keys_values, hidden, w_router, routed, core, split, wide
    )
    block = jnp.stack([sent[0]] + [across(part, 1) for part in sent[1:]])
    arrived = {k: across(block, k) for k in far_first}
    blocks = [block] + [arrived[k] for k in range(split, seq, split)]
    logit = logit_part
    if split == 2:
        logit = jnp.concatenate([logit_part, across(logit_part, 1)], axis=0)
    logits = [logit] + [around(logit, k) for k in range(1, tp)]
    rows = [chosen_x] + [across(chosen_x, 1)] * (split - 1)
    parts = gather_queries(queries, routed, grad_out, core, split, [block, logit])
    sides = [parts[0]] + [across(part, 1) for part in parts[1:]]

    results = attend(plan, shard, counts, blocks, sides, logits)
    outs, backs, gate = results[:split], results[split:-1], results[-1]
    gates = [gate] + [around(gate, k) for k in range(1, tp)]
    returned = {k: across(backs[k // split], k) for k in far_first}
    if split == 1:
        branch_out, grad_queries = outs[0][0], outs[0][1]
    else:
        taken = across(outs[1], 1)
        branch_out, grad_queries = join_halves(core, outs[0], taken)
    router = router_part(shard, counts, logits, gates, rows, wide, [branch_out])
    if split == 2:
        router = router + across(router, 1)
    routers = [router] + [across(router, k) for k in far_first]
    sums = add_up([backs[0]] + [returned[k] for k in far_first], [router])
    if split == 1:
        grad_keys_values, grad_router = sums[0], sum(routers)
    else:
        grad_keys_values, grad_router = finish(core, sums[0], across(sums[1], 1), routers)
    return (branch_out, grad_queries, grad_keys_values, grad_router.reshape(-1))


def solution(mesh):
    in_specs = (
        P("seq", "tp"),
        P("seq", "tp"),
        P(None, "seq", "tp"),
        P("tp"),
        P("seq", None),
        P(),
        P("seq", "tp"),
    )
    out_specs = (P("seq", "tp"), P("seq", "tp"), P(None, "seq", "tp"), P("tp"))

    return jax.shard_map(shards, mesh=mesh, in_specs=in_specs, out_specs=out_specs, check_vma=False)
```

```python
import functools
import math

import jax
import jax.numpy as jnp
from jax import lax
from jax.experimental import pallas as pl
from jax.experimental.pallas import tpu as pltpu
from jax.sharding import PartitionSpec as P


HEAD_WIDTH = 128
LANES = 128
LOG2E = math.log2(math.e)
FAR = 1 << 30
BF16 = jnp.bfloat16
F32 = jnp.float32


def dot(a, b):
    return lax.dot_general(a, b, (((1,), (0,)), ((), ())), preferred_element_type=F32)


def eye(shape):
    return lax.broadcasted_iota(jnp.int32, shape, 0) == lax.broadcasted_iota(jnp.int32, shape, 1)


def row_to_column(row, rows):
    spread = jnp.broadcast_to(row, (rows, row.shape[1]))
    return jnp.sum(jnp.where(eye(spread.shape), spread, 0.0), axis=1, keepdims=True)


def column_to_row(column, width):
    spread = jnp.broadcast_to(column, (column.shape[0], width))
    return jnp.sum(jnp.where(eye(spread.shape), spread, 0.0), axis=0, keepdims=True)


def one_hot(routed_row, tokens):
    slots = routed_row.shape[1]
    column = row_to_column(routed_row.astype(F32), slots).astype(jnp.int32)
    ids = lax.broadcasted_iota(jnp.int32, (slots, tokens), 1)
    return jnp.where(ids == column, 1.0, 0.0).astype(BF16)


def rows_of(split, core, rows):
    if split == 1:
        return [rows]
    low, high = rows[:, :HEAD_WIDTH], rows[:, HEAD_WIDTH:]
    first = core == 0
    return [jnp.where(first, low, high), jnp.where(first, high, low)]


VMEM = pl.BlockSpec(memory_space=pltpu.VMEM)
ANYWHERE = pl.BlockSpec(memory_space=pl.ANY)
SMALL = pltpu.CompilerParams(vmem_limit_bytes=16 << 20)


HBM = pl.BlockSpec(memory_space=pltpu.HBM)


def in_hbm(*arrays):
    return [pltpu.with_memory_space_constraint(array, pltpu.HBM) for array in arrays]


def gather_first(keys_values, hidden, w_router, routed, core, split, wide):
    tokens, model = hidden.shape
    slots = routed.shape[1]
    step = 256
    parts = 4 if model % (4 * step) == 0 else 1
    part = model // parts
    weights = w_router.reshape(model // LANES, LANES)

    def body(core_ref, routed_hbm, w_hbm, kv_hbm, x_hbm, *refs):
        outs, (x_out, logit_ref) = refs[:split], refs[split : split + 2]
        routed_buf, w_buf, kv_buf, x_buf, sem, x_sem = refs[split + 2 :]
        fetch = pltpu.make_async_copy(routed_hbm, routed_buf, sem.at[2])
        fetch_w = pltpu.make_async_copy(w_hbm, w_buf, sem.at[3])
        copies = [
            pltpu.make_async_copy(kv_hbm.at[i], kv_buf.at[i], sem.at[i]) for i in range(2)
        ]
        x_copies = [
            pltpu.make_async_copy(
                x_hbm.at[:, pl.ds(p * part, part)], x_buf.at[:, pl.ds(p * part, part)], x_sem.at[p]
            )
            for p in range(parts)
        ]
        for copy in [fetch, fetch_w] + copies + x_copies:
            copy.start()
        fetch.wait()
        select = one_hot(routed_buf[...], tokens)
        for i in range(2):
            copies[i].wait()
            rows = dot(select, kv_buf[i]).astype(BF16)
            for out, rows_part in zip(outs, rows_of(split, core_ref[0], rows)):
                out[i] = rows_part
        fetch_w.wait()
        acc = jnp.zeros((slots, LANES), F32)
        for p in range(parts):
            x_copies[p].wait()
            for j in range(p * part // step, (p + 1) * part // step):
                rows = dot(select, x_buf[:, j * step : (j + 1) * step])
                x_out[:, j * step : (j + 1) * step] = rows.astype(BF16)
                for t in range(step // LANES):
                    b = j * (step // LANES) + t
                    weight = w_buf[b : b + 1, :].astype(F32)
                    acc = acc + rows[:, t * LANES : (t + 1) * LANES] * weight
        logit_ref[...] = column_to_row(jnp.sum(acc, axis=1, keepdims=True), wide)

    return pl.pallas_call(
        body,
        grid_spec=pltpu.PrefetchScalarGridSpec(
            num_scalar_prefetch=1,
            grid=(1,),
            in_specs=[HBM] * 4,
            out_specs=[VMEM] * (split + 2),
            scratch_shapes=[
                pltpu.VMEM(routed.shape, jnp.int32),
                pltpu.VMEM(weights.shape, BF16),
                pltpu.VMEM(keys_values.shape, BF16),
                pltpu.VMEM(hidden.shape, BF16),
                pltpu.SemaphoreType.DMA((4,)),
                pltpu.SemaphoreType.DMA((parts,)),
            ],
        ),
        out_shape=[jax.ShapeDtypeStruct((2, slots, HEAD_WIDTH), BF16)] * split
        + [
            jax.ShapeDtypeStruct((slots, model), BF16),
            jax.ShapeDtypeStruct((1, wide), F32),
        ],
        compiler_params=SMALL,
        name="gather_first",
    )(core, *in_hbm(routed, weights, keys_values, hidden))


def gather_queries(queries, routed, grad_out, core, split, after):
    tokens, width = queries.shape
    slots = routed.shape[1]
    half = width // split
    step = 256

    def body(core_ref, routed_ref, g_ref, q_ref, *refs):
        outs = refs[len(after) :]
        select = one_hot(routed_ref[...], tokens)
        for o in range(split):
            start = pl.multiple_of((core_ref[0] ^ o) % split * half, half)
            outs[o][1] = g_ref[:, pl.ds(start, half)]
            for j in range(half // step):
                at = pl.ds(pl.multiple_of(start + j * step, step), step)
                rows = dot(select, q_ref[:, at]).astype(BF16)
                outs[o][0, :, j * step : (j + 1) * step] = rows

    return pl.pallas_call(
        body,
        grid_spec=pltpu.PrefetchScalarGridSpec(
            num_scalar_prefetch=1,
            grid=(1,),
            in_specs=[VMEM] * 3 + [ANYWHERE] * len(after),
            out_specs=[VMEM] * split,
        ),
        out_shape=[jax.ShapeDtypeStruct((2, slots, half), BF16)] * split,
        compiler_params=SMALL,
        name="gather_queries",
    )(core, routed, grad_out, queries, *after)


class Plan:
    def __init__(self, seq, split, slots, group, wide):
        self.seq, self.split, self.slots, self.group, self.wide = seq, split, slots, group, wide
        self.tile = 256
        self.tiles = -(-seq * slots // self.tile)
        self.keys = self.tiles * self.tile
        self.rows = 32
        self.chunks = slots // self.rows
        self.lanes = self.rows * group
        self.blocks = seq // split


def stack_heads(block, plan):
    return jnp.concatenate(
        [block[:, h * HEAD_WIDTH : (h + 1) * HEAD_WIDTH] for h in range(plan.group)], axis=0
    )


def total_of(refs, side):
    total = refs[0][side : side + 1, :]
    for ref in refs[1:]:
        total = total + ref[side : side + 1, :]
    return total


def gate_of(logit):
    return 1.0 / (1.0 + jnp.exp(-logit))


def repeat(tiles, step, carried):
    if isinstance(tiles, int):
        for t in range(tiles):
            carried = step(t, carried)
        return carried
    return lax.fori_loop(0, tiles, step, carried)


def attend(plan, shard, counts, blocks, sides, logits):
    seq, split, slots, tile, lanes = plan.seq, plan.split, plan.slots, plan.tile, plan.lanes
    inverse = 1.0 / math.sqrt(HEAD_WIDTH)
    scale = LOG2E * inverse
    reps = lanes // LANES
    width = plan.group * HEAD_WIDTH

    def body(shard_ref, counts_ref, *refs):
        refs = list(refs)
        block_refs = [refs.pop(0) for _ in range(plan.blocks)]
        side_refs = [refs.pop(0) for _ in range(split)]
        logit_refs = [refs.pop(0) for _ in range(len(logits))]
        out_refs = [refs.pop(0) for _ in range(split)]
        back_refs = [refs.pop(0) for _ in range(plan.blocks)]
        gate_ref = refs.pop(0)
        (keys, values, place, keys_t, values_t, scores, pulls) = refs[:7]
        (key_acc, value_acc, columns, gate_column, starts) = refs[7:]
        own = shard_ref[0]
        end = jnp.int32(0)
        for j in range(seq):
            starts[j] = end
            end = end + ((counts_ref[j] + 15) // 16) * 16
        for b in range(plan.blocks):
            for i in range(split):
                source = own ^ (b * split + i)
                live = counts_ref[source]
                start = starts[source]

                def move(t, _, b=b, i=i, live=live, start=start):
                    at = pl.multiple_of(t * 16, 16)
                    to = pl.multiple_of(start + t * 16, 16)
                    keys[pl.ds(to, 16), :] = block_refs[b][i, 0, pl.ds(at, 16), :]
                    values[pl.ds(to, 16), :] = block_refs[b][i, 1, pl.ds(at, 16), :]
                    slot = at + lax.broadcasted_iota(jnp.int32, (16, LANES), 0)
                    place[pl.ds(to, 16), :] = jnp.where(slot < live, start + slot, FAR)
                    return 0

                lax.fori_loop(0, (live + 15) // 16, move, 0)
        tail = pl.ds(pl.multiple_of(end, 16), tile)
        keys[tail, :] = jnp.zeros((tile, HEAD_WIDTH), BF16)
        values[tail, :] = jnp.zeros((tile, HEAD_WIDTH), BF16)
        place[tail, :] = jnp.full((tile, LANES), FAR, jnp.int32)

        def prepare(t, _):
            here = pl.ds(pl.multiple_of(t * tile, tile), tile)
            keys_t[:, here] = keys[here, :].T
            values_t[:, here] = values[here, :].T
            key_acc[here, :] = jnp.zeros((tile, HEAD_WIDTH), F32)
            value_acc[here, :] = jnp.zeros((tile, HEAD_WIDTH), F32)
            return 0

        lax.fori_loop(0, (end + tile - 1) // tile, prepare, 0)
        gate_column[...] = jnp.zeros_like(gate_column)
        for side in range(split):
            weight = gate_of(total_of(logit_refs, side))
            slot = lax.broadcasted_iota(jnp.int32, weight.shape, 1)
            weight = jnp.where(slot < counts_ref[own ^ side], weight, 0.0)
            for b in range(plan.wide // LANES):
                at = slice(b * LANES, (b + 1) * LANES)
                column = row_to_column(weight[:, at], LANES)
                columns[side, at, :] = jnp.broadcast_to(column, (LANES, LANES))

        def chunk_step(side, chunk, _):
            mine = own ^ side
            live = counts_ref[mine]
            offset = starts[mine]
            first = pl.multiple_of(chunk * plan.rows, plan.rows)
            at = pl.ds(first, plan.rows)
            needed = (offset + jnp.minimum(live, first + plan.rows) + tile - 1) // tile
            needed = jnp.where(first < live, needed, 0)

            @pl.when(needed == 0)
            def _():
                out_refs[side][:, at, :] = jnp.zeros((2, plan.rows, width), BF16)

            def work(tiles):
                q = stack_heads(side_refs[side][0, at, :], plan)
                upstream = stack_heads(side_refs[side][1, at, :], plan).astype(F32)
                weight = jnp.concatenate([columns[side, at, :]] * plan.group, axis=0)
                narrow = (upstream * weight).astype(BF16)
                q_t = q.T
                narrow_t = narrow.T
                lane = lax.broadcasted_iota(jnp.int32, (1, lanes), 1)
                positions = offset + first + lane % plan.rows

                def here_of(t):
                    if isinstance(t, int):
                        return slice(t * tile, (t + 1) * tile)
                    return pl.ds(pl.multiple_of(t * tile, tile), tile)

                def score(t, running):
                    here = here_of(t)
                    s = dot(keys[here, :], q_t) * scale
                    allowed = jnp.concatenate([place[here, :]] * reps, axis=1) <= positions
                    s = jnp.where(allowed, s, -jnp.inf)
                    scores[here, :] = s
                    pulls[here, :] = dot(values[here, :], narrow_t)
                    return jnp.maximum(running, jnp.max(s, axis=0, keepdims=True))

                top = repeat(tiles, score, jnp.full((1, lanes), -1e30, F32))

                def spread(t, carried):
                    summed, out_t = carried
                    here = here_of(t)
                    p = jnp.exp2(scores[here, :] - top)
                    scores[here, :] = p
                    summed = summed + jnp.sum(p, axis=0, keepdims=True)
                    return (summed, out_t + dot(values_t[:, here], p.astype(BF16)))

                summed, out_t = repeat(
                    tiles,
                    spread,
                    (jnp.zeros((1, lanes), F32), jnp.zeros((HEAD_WIDTH, lanes), F32)),
                )
                share = 1.0 / summed
                out_t = out_t * share
                delta = jnp.sum(narrow_t.astype(F32) * out_t, axis=0, keepdims=True)

                def back(t, grad_t):
                    here = here_of(t)
                    p = scores[here, :] * share
                    dp = pulls[here, :]
                    value_acc[here, :] += dot(p.astype(BF16), narrow)
                    ds = (p * (dp - delta)).astype(BF16)
                    key_acc[here, :] += dot(ds, q)
                    return grad_t + dot(keys_t[:, here], ds)

                grad_t = repeat(tiles, back, jnp.zeros((HEAD_WIDTH, lanes), F32))
                out = out_t.T
                raw = upstream * out
                gate = raw[: plan.rows]
                for h in range(1, plan.group):
                    gate = gate + raw[h * plan.rows : (h + 1) * plan.rows]
                gate_column[side, at, :] = gate
                weighted = (out * weight).astype(BF16)
                grad = (grad_t * inverse).astype(BF16).T
                for h in range(plan.group):
                    heads = slice(h * HEAD_WIDTH, (h + 1) * HEAD_WIDTH)
                    rows = slice(h * plan.rows, (h + 1) * plan.rows)
                    out_refs[side][0, at, heads] = weighted[rows]
                    out_refs[side][1, at, heads] = grad[rows]

            if plan.tiles <= 5:
                for tiles in range(1, plan.tiles + 1):
                    pl.when(needed == tiles)(functools.partial(work, tiles))
            else:
                pl.when(needed > 0)(functools.partial(work, needed))
            return 0

        for side in range(split):
            lax.fori_loop(0, plan.chunks, functools.partial(chunk_step, side), 0)
        for side in range(split):
            gate_ref[side : side + 1, :] = column_to_row(
                jnp.sum(gate_column[side], axis=1, keepdims=True), plan.wide
            )
        for b in range(plan.blocks):
            back_refs[b][...] = jnp.zeros_like(back_refs[b])
            for i in range(split):
                source = own ^ (b * split + i)
                live = counts_ref[source]
                start = starts[source]

                def give(t, _, b=b, i=i, start=start):
                    at = pl.ds(pl.multiple_of(t * 16, 16), 16)
                    here = pl.ds(pl.multiple_of(start + t * 16, 16), 16)
                    back_refs[b][i, 0, at, :] = (key_acc[here, :] * inverse).astype(BF16)
                    back_refs[b][i, 1, at, :] = value_acc[here, :].astype(BF16)
                    return 0

                lax.fori_loop(0, (live + 15) // 16, give, 0)

    block = (split, 2, slots, HEAD_WIDTH)
    side = (2, slots, width)
    return pl.pallas_call(
        body,
        grid_spec=pltpu.PrefetchScalarGridSpec(
            num_scalar_prefetch=2,
            grid=(1,),
            in_specs=[VMEM] * plan.blocks
            + [VMEM] * (split + len(logits)),
            out_specs=[VMEM] * (split + plan.blocks + 1),
            scratch_shapes=[
                pltpu.VMEM((plan.keys + tile, HEAD_WIDTH), BF16),
                pltpu.VMEM((plan.keys + tile, HEAD_WIDTH), BF16),
                pltpu.VMEM((plan.keys + tile, LANES), jnp.int32),
                pltpu.VMEM((HEAD_WIDTH, plan.keys), BF16),
                pltpu.VMEM((HEAD_WIDTH, plan.keys), BF16),
                pltpu.VMEM((plan.keys, lanes), F32),
                pltpu.VMEM((plan.keys, lanes), F32),
                pltpu.VMEM((plan.keys, HEAD_WIDTH), F32),
                pltpu.VMEM((plan.keys, HEAD_WIDTH), F32),
                pltpu.VMEM((split, plan.wide, LANES), F32),
                pltpu.VMEM((split, slots, LANES), F32),
                pltpu.SMEM((seq,), jnp.int32),
            ],
        ),
        out_shape=[jax.ShapeDtypeStruct(side, BF16)] * split
        + [jax.ShapeDtypeStruct(block, BF16)] * plan.blocks
        + [jax.ShapeDtypeStruct((split, plan.wide), F32)],
        compiler_params=pltpu.CompilerParams(
            vmem_limit_bytes=(24 << 20) if plan.tiles <= 5 else (48 << 20)
        ),
        name="attend",
    )(shard, counts, *blocks, *sides, *logits)


def router_part(shard, counts, logits, gates, rows):
    slots, width = rows[0].shape
    split = len(rows)
    number = len(logits)

    def body(shard_ref, counts_ref, *refs):
        logit_refs, gate_refs = refs[:number], refs[number : 2 * number]
        row_refs, out_ref = refs[2 * number : 2 * number + split], refs[-1]
        columns = []
        for side in range(split):
            gate = gate_of(total_of(logit_refs, side))
            term = total_of(gate_refs, side)
            slot = lax.broadcasted_iota(jnp.int32, gate.shape, 1)
            live = slot < counts_ref[shard_ref[0] ^ side]
            columns.append(
                jnp.broadcast_to(
                    row_to_column(jnp.where(live, term * gate * (1.0 - gate), 0.0), slots),
                    (slots, LANES),
                )
            )
        for b in range(width // LANES):
            at = slice(b * LANES, (b + 1) * LANES)
            product = row_refs[0][:, at].astype(F32) * columns[0]
            for side in range(1, split):
                product = product + row_refs[side][:, at].astype(F32) * columns[side]
            out_ref[b : b + 1, :] = jnp.sum(product, axis=0, keepdims=True)

    return pl.pallas_call(
        body,
        grid_spec=pltpu.PrefetchScalarGridSpec(
            num_scalar_prefetch=2,
            grid=(1,),
            in_specs=[VMEM] * (2 * number + split),
            out_specs=VMEM,
        ),
        out_shape=jax.ShapeDtypeStruct((width // LANES, LANES), F32),
        compiler_params=SMALL,
        name="router_part",
    )(shard, counts, *logits, *gates, *rows)


def join_halves(core, mine, taken):
    _, slots, half = mine.shape

    def body(core_ref, mine_ref, taken_ref, *outs):
        for a in range(2):
            @pl.when(pl.program_id(0) == 0)
            def _(a=a):
                outs[a][...] = mine_ref[a]

            @pl.when(pl.program_id(0) == 1)
            def _(a=a):
                outs[a][...] = taken_ref[a]

    return pl.pallas_call(
        body,
        grid_spec=pltpu.PrefetchScalarGridSpec(
            num_scalar_prefetch=1,
            grid=(2,),
            in_specs=[VMEM] * 2,
            out_specs=[pl.BlockSpec((slots, half), lambda i, c: (0, i ^ c[0]))] * 2,
        ),
        out_shape=[jax.ShapeDtypeStruct((slots, 2 * half), BF16)] * 2,
        compiler_params=SMALL,
        name="join_halves",
    )(core, mine, taken)


def add_up(blocks):
    split = blocks[0].shape[0]
    number = len(blocks)
    shape = blocks[0].shape[1:]

    def body(*refs):
        ins, outs = refs[:number], refs[number:]
        for side in range(split):
            acc = ins[0][side].astype(F32)
            for ref in ins[1:]:
                acc = acc + ref[side].astype(F32)
            outs[side][...] = acc.astype(BF16)

    return pl.pallas_call(
        body,
        grid=(1,),
        in_specs=[VMEM] * number,
        out_specs=[VMEM] * split,
        out_shape=[jax.ShapeDtypeStruct(shape, BF16)] * split,
        compiler_params=SMALL,
        name="add_up",
    )(*blocks)


def finish(core, mine, taken, routers):
    _, slots, head = mine.shape
    number = len(routers)

    def body(core_ref, mine_ref, taken_ref, *refs):
        out_ref, router_out = refs[number:]
        first = core_ref[0] == 0
        a, b = mine_ref[...], taken_ref[...]
        out_ref[:, :, :head] = jnp.where(first, a, b)
        out_ref[:, :, head:] = jnp.where(first, b, a)
        total = refs[0][...]
        for ref in refs[1:number]:
            total = total + ref[...]
        router_out[...] = total

    return pl.pallas_call(
        body,
        grid_spec=pltpu.PrefetchScalarGridSpec(
            num_scalar_prefetch=1,
            grid=(1,),
            in_specs=[VMEM] * (2 + number),
            out_specs=[VMEM] * 2,
        ),
        out_shape=[
            jax.ShapeDtypeStruct((2, slots, 2 * head), BF16),
            jax.ShapeDtypeStruct(routers[0].shape, F32),
        ],
        compiler_params=SMALL,
        name="finish",
    )(core, mine, taken, *routers)


def shards(hidden, queries, keys_values, w_router, routed, counts, grad_out):
    seq = lax.axis_size("seq")
    tp = lax.axis_size("tp")
    slots = routed.shape[1]
    kv_local = keys_values.shape[2] // HEAD_WIDTH
    q_local = queries.shape[1] // HEAD_WIDTH
    group = q_local // kv_local
    split = 2 if kv_local == 2 else 1
    wide = -(-slots // LANES) * LANES
    if kv_local != split or seq & (seq - 1) or slots % 32 or group * 32 % LANES:
        raise ValueError("unsupported sizes")
    plan = Plan(seq, split, slots, group, wide)
    own = lax.axis_index("seq").astype(jnp.int32)
    shard = own.reshape(1)
    core = (own % 2).reshape(1)

    def across(value, k):
        return lax.ppermute(value, "seq", [(i, i ^ k) for i in range(seq)])

    def around(value, k):
        if tp & (tp - 1):
            return lax.ppermute(value, "tp", [(i, (i + k) % tp) for i in range(tp)])
        return lax.ppermute(value, "tp", [(i, i ^ k) for i in range(tp)])

    far_first = sorted(range(split, seq, split), key=lambda k: -bin(k).count("1"))

    *sent, chosen_x, logit_part = gather_first(
        keys_values, hidden, w_router, routed, core, split, wide
    )
    block = jnp.stack([sent[0]] + [across(part, 1) for part in sent[1:]])
    arrived = {k: across(block, k) for k in far_first}
    blocks = [block] + [arrived[k] for k in range(split, seq, split)]
    logit = logit_part
    if split == 2:
        logit = jnp.concatenate([logit_part, across(logit_part, 1)], axis=0)
    logits = [logit] + [around(logit, k) for k in range(1, tp)]
    rows = [chosen_x] + [across(chosen_x, 1)] * (split - 1)
    queries, grad_out, _ = lax.optimization_barrier((queries, grad_out, logit_part))
    parts = gather_queries(queries, routed, grad_out, core, split, [block, logit])
    sides = [parts[0]] + [across(part, 1) for part in parts[1:]]

    results = attend(plan, shard, counts, blocks, sides, logits)
    outs, backs, gate = results[:split], results[split:-1], results[-1]
    gates = [gate] + [around(gate, k) for k in range(1, tp)]
    returned = {k: across(backs[k // split], k) for k in far_first}
    if split == 1:
        branch_out, grad_queries = outs[0][0], outs[0][1]
    else:
        taken = across(outs[1], 1)
        branch_out, grad_queries = join_halves(core, outs[0], taken)
    router = router_part(shard, counts, logits, gates, rows)
    if split == 2:
        router = router + across(router, 1)
    routers = [router] + [across(router, k) for k in far_first]
    sums = add_up([backs[0]] + [returned[k] for k in far_first])
    if split == 1:
        grad_keys_values, grad_router = sums[0], sum(routers)
    else:
        grad_keys_values, grad_router = finish(core, sums[0], across(sums[1], 1), routers)
    return (branch_out, grad_queries, grad_keys_values, grad_router.reshape(-1))


def solution(mesh):
    in_specs = (
        P("seq", "tp"),
        P("seq", "tp"),
        P(None, "seq", "tp"),
        P("tp"),
        P("seq", None),
        P(),
        P("seq", "tp"),
    )
    out_specs = (P("seq", "tp"), P("seq", "tp"), P(None, "seq", "tp"), P("tp"))

    return jax.shard_map(shards, mesh=mesh, in_specs=in_specs, out_specs=out_specs, check_vma=False)
```
